32 devices in a mesh: layer: 2 (over x), feat: 4 (over z), tok: 4 (over y, core).
Axes of the slice: x: 2, y: 2, z: 4, core: 2. Of those that a mesh axis runs over, the one named last changes fastest.
Arguments:
- resid: bfloat16 [2, 1024, 2304], P('layer', 'tok', 'feat'), may hold values from -6 to 6
- norm_gain: bfloat16 [2, 2304], P('layer', 'feat'), may hold values from 0.5 to 2
- prev_codes: bfloat16 [1024, 16384], P('tok', 'feat'), may hold values from 0 to 1.5
- feature_mask: int32 [2, 8, 128], P('layer', 'tok', 'feat'), may hold values 0 or 1
- w_gate: bfloat16 [2, 2304, 9216], P('layer', 'tok', 'feat'), may hold values from -0.125 to 0.125
- w_up: bfloat16 [2, 2304, 9216], P('layer', 'tok', 'feat'), may hold values from -0.125 to 0.125
- w_down: bfloat16 [2, 9216, 2304], P('layer', 'feat', 'tok'), may hold values from -0.0625 to 0.0625
- enc_weight: bfloat16 [2, 2304, 16384], P('layer', 'tok', 'feat'), may hold values from -0.125 to 0.125
- enc_bias: float32 [2, 16384], P('layer', 'feat'), may hold values from -3 to 3
- dec_own: bfloat16 [2, 16384, 2304], P('layer', 'feat', 'tok'), may hold values from -0.046875 to 0.046875
- dec_prev: bfloat16 [2, 16384, 2304], P('layer', 'feat', 'tok'), may hold values from -0.046875 to 0.046875
Outputs:
- grad_enc: float32 [2, 2304, 16384], P('layer', 'tok', 'feat')
- grad_bias: float32 [2, 16384], P('layer', 'feat')
- grad_own: float32 [2, 16384, 2304], P('layer', 'feat', 'tok')
- grad_prev: float32 [2, 16384, 2304], P('layer', 'feat', 'tok')
The draws below stay inside these ranges and needn't reach their ends.
All inputs are finite; a program needn't handle non-finite values. No bound on the sum of `feature_mask` on one device may be relied on, other than what follows from the above.
Results may differ from the reference program's by a relative error of at most 0.0063.
Values may be sent and summed in bfloat16 or wider, within the bound.
A program may use at most 256 MiB of HBM per device.

```python
import math
import jax
import jax.numpy as jnp
from jax import lax

D = 2304
FF = 9216
F = 16384
TILE = 128
TBLK = 128
TOKENS = 1024
LAYERS = 2


def with_ends(values, rng, least, high):
    longest = values.shape.index(max(values.shape))
    spots = []
    for shift in (0, 1):
        where = [jax.random.randint(jax.random.fold_in(rng, axis), (), 0, length) for axis, length in enumerate(values.shape)]
        where[longest] = (where[longest] + shift) % values.shape[longest]
        spots.append(tuple(where))
    return values.at[spots[0]].set(least).at[spots[1]].set(high)


def steps_of(own_key, shape, pieces, smallest, top_value):
    gain = 1.0
    for axis_at, parts in pieces:
        heights = jax.random.uniform(jax.random.fold_in(jax.random.fold_in(own_key, 6), axis_at), (parts,), jnp.float32, smallest / len(pieces), top_value / len(pieces))
        gain = gain * jnp.repeat(jnp.exp(heights), shape[axis_at] // parts).reshape((-1,) + (1,) * (len(shape) - 1 - axis_at))
    return gain


def gaussian(key, shape, deviation, limit, shards=(), held_as=jnp.bfloat16):
    entries = deviation * jax.random.normal(key, shape, jnp.float32)
    if shards:
        entries = entries * steps_of(key, shape, shards, -0.22, 0.18)
    return jnp.clip(entries, -limit, limit).astype(held_as)


def setup_inputs(seed: int = 0) -> dict:
    key_of = jax.random.split(jax.random.key(seed), 12)
    return {
        "resid": gaussian(key_of[0], (LAYERS, TOKENS, D), 1.0, 6.0, ((0, 2), (1, 4), (2, 4))),
        "norm_gain": jnp.clip(0.5 + 1.5 * jax.random.uniform(key_of[1], (LAYERS, D), jnp.float32) ** steps_of(key_of[1], (LAYERS, D), ((0, 2), (1, 4)), -0.2, 0.2), 0.5, 2.0).astype(jnp.bfloat16),
        "prev_codes": jnp.clip(1.5 * jax.random.uniform(key_of[2], (TOKENS, F), jnp.float32) ** steps_of(key_of[2], (TOKENS, F), ((0, 4), (1, 4)), -0.2, 0.2), 0.0, 1.5).astype(jnp.bfloat16),
        "feature_mask": with_ends((jax.random.randint(key_of[3], (LAYERS, TOKENS // TBLK, F // TILE), 0, 4) < 3).astype(jnp.int32), jax.random.fold_in(key_of[3], 1), 0, 1),
        "w_gate": gaussian(key_of[4], (LAYERS, D, FF), D ** -0.5, 0.125, ((0, 2), (1, 4), (2, 4))),
        "w_up": gaussian(key_of[5], (LAYERS, D, FF), D ** -0.5, 0.125, ((0, 2), (1, 4), (2, 4))),
        "w_down": gaussian(key_of[6], (LAYERS, FF, D), FF ** -0.5, 0.0625, ((0, 2), (1, 4), (2, 4))),
        "enc_weight": gaussian(key_of[7], (LAYERS, D, F), D ** -0.5, 0.125, ((0, 2), (1, 4), (2, 4))),
        "enc_bias": gaussian(key_of[8], (LAYERS, F), 0.5, 3.0, ((0, 2), (1, 4)), jnp.float32),
        "dec_own": gaussian(key_of[9], (LAYERS, F, D), F ** -0.5, 0.046875, ((0, 2), (1, 4), (2, 4))),
        "dec_prev": gaussian(key_of[10], (LAYERS, F, D), F ** -0.5, 0.046875, ((0, 2), (1, 4), (2, 4))),
    }


def expand_mask(block_mask):
    grown = jnp.repeat(jnp.repeat(block_mask, TBLK, axis=0), TILE, axis=1)
    return grown.astype(jnp.float32)

def reference(resid, norm_gain, prev_codes, feature_mask, w_gate, w_up, w_down, enc_weight, enc_bias, dec_own, dec_prev):
    factor = 1.0 / math.sqrt(TOKENS)
    normed_list = []
    codes_list = []
    source_list = []
    active_list = []
    keeper_list = []
    error_list = []
    for layer_idx in range(LAYERS):
        stream = resid[layer_idx].astype(jnp.float32)
        normed = (stream * lax.rsqrt(lax.optimization_barrier(jnp.mean(stream * stream, axis=1, keepdims=True)) + 1e-06) * norm_gain[layer_idx].astype(jnp.float32)).astype(jnp.bfloat16)
        gate_sum = jnp.dot(normed, w_gate[layer_idx], preferred_element_type=jnp.float32)
        up_sum = jnp.dot(normed, w_up[layer_idx], preferred_element_type=jnp.float32)
        hidden = (jax.nn.gelu(gate_sum, approximate=True) * up_sum).astype(jnp.bfloat16)
        preact = jnp.dot(normed, enc_weight[layer_idx], preferred_element_type=jnp.float32) + enc_bias[layer_idx]
        active = jnp.maximum(preact, 0.0)
        keeper = expand_mask(feature_mask[layer_idx])
        codes = (active * active * keeper).astype(jnp.bfloat16)
        source = prev_codes if layer_idx == 0 else codes_list[-1]
        partial_value = jnp.dot(codes, dec_own[layer_idx], preferred_element_type=jnp.float32) + jnp.dot(source, dec_prev[layer_idx], preferred_element_type=jnp.float32) - jnp.dot(hidden, w_down[layer_idx], preferred_element_type=jnp.float32)
        normed_list.append(normed)
        codes_list.append(codes)
        source_list.append(source)
        active_list.append(active)
        keeper_list.append(keeper)
        error_list.append(partial_value.astype(jnp.bfloat16))
    grads_enc = []
    grads_bias = []
    grads_own = []
    grads_prev = []
    for layer_idx in range(LAYERS):
        error = error_list[layer_idx]
        back = jnp.dot(error, dec_own[layer_idx].T, preferred_element_type=jnp.float32)
        if layer_idx + 1 < LAYERS:
            back = back + jnp.dot(error_list[layer_idx + 1], dec_prev[layer_idx + 1].T, preferred_element_type=jnp.float32)
        pregrad = (back * keeper_list[layer_idx] * (2.0 * active_list[layer_idx]) * factor).astype(jnp.bfloat16)
        grads_enc.append(jnp.dot(normed_list[layer_idx].T, pregrad, preferred_element_type=jnp.float32))
        grads_bias.append(lax.optimization_barrier(jnp.sum(pregrad.astype(jnp.float32), axis=0)))
        grads_own.append(jnp.dot(codes_list[layer_idx].T, error, preferred_element_type=jnp.float32) * factor)
        grads_prev.append(jnp.dot(source_list[layer_idx].T, error, preferred_element_type=jnp.float32) * factor)
    return (jnp.stack(grads_enc), jnp.stack(grads_bias), jnp.stack(grads_own), jnp.stack(grads_prev))
```

```python
import math

import jax
import jax.numpy as jnp
from jax import lax
from jax.sharding import PartitionSpec as P

TILE = 128
TBLK = 128


def passed_along(value, axis, steps):
    count = lax.axis_size(axis)
    leading, last = (max(0, -steps), min(count, count - steps))
    return lax.ppermute(value, axis, [(source, source + steps) for source in range(leading, last)])


def swapped(value, axis, bit):
    return lax.ppermute(value, axis, [(i, i ^ bit) for i in range(lax.axis_size(axis))])


def levels(axis):
    return [1 << k for k in range(lax.axis_size(axis).bit_length() - 1)]


def relative_blocks(axis):
    order = [0]
    for bit in reversed(levels(axis)):
        order += [r ^ bit for r in order]
    return order


def spread_blocks(value, axis):
    for bit in reversed(levels(axis)):
        value = jnp.concatenate([value, swapped(value, axis, bit)], axis=0)
    return value


def summed_block(product, rows, axis):
    first, *others = levels(axis)
    half = rows.shape[0] // 2
    away = product(rows[half:]).astype(jnp.bfloat16)
    total = product(rows[:half]) + swapped(away, axis, first).astype(jnp.float32)
    for bit in others:
        half = total.shape[0] // 2
        away = total[half:].astype(jnp.bfloat16)
        total = total[:half] + swapped(away, axis, bit).astype(jnp.float32)
    return total


def block_keep(block_mask, height, breadth):
    blocks = block_mask.astype(jnp.float32)
    spread = jnp.broadcast_to(
        blocks[:, None, :, None], (blocks.shape[0], TBLK, blocks.shape[1], TILE)
    )
    return spread.reshape(height, breadth)


def local(
    resid,
    norm_gain,
    prev_codes,
    feature_mask,
    w_gate,
    w_up,
    w_down,
    enc_weight,
    enc_bias,
    dec_own,
    dec_prev,
):
    gathered, gains = (
        lax.all_gather(resid[0], "feat", axis=1, tiled=True),
        lax.all_gather(norm_gain, "feat", axis=1, tiled=True),
    )
    stream = gathered.astype(jnp.float32)
    normed = (
        stream
        * lax.rsqrt(jnp.mean(stream * stream, axis=1, keepdims=True) + 1e-06)
        * gains[0].astype(jnp.float32)
    ).astype(jnp.bfloat16)
    height = normed.shape[0]
    width = enc_weight.shape[1]
    feat_local = enc_weight.shape[2]
    here = lax.axis_index("tok")
    pieces = []
    for r in relative_blocks("tok"):
        piece = lax.dynamic_slice_in_dim(normed, (here ^ r) * width, width, axis=1)
        pieces.append(swapped(piece, "tok", r) if r else piece)
    normed_cols = jnp.concatenate(pieces, axis=0)

    def times(weight):
        return lambda rows: jnp.dot(rows, weight, preferred_element_type=jnp.float32)

    enc_sum = summed_block(times(enc_weight[0]), normed_cols, "tok")
    gate_sum = summed_block(times(w_gate[0]), normed_cols, "tok")
    up_sum = summed_block(times(w_up[0]), normed_cols, "tok")
    hidden = (jax.nn.gelu(gate_sum, approximate=True) * up_sum).astype(jnp.bfloat16)
    preact = enc_sum + enc_bias[0]
    active = jnp.maximum(preact, 0.0)
    keeper = block_keep(feature_mask[0], height, feat_local)
    codes = (active * active * keeper).astype(jnp.bfloat16)
    shifted = passed_along(codes, "layer", 1)
    source = jnp.where(lax.axis_index("layer") == 0, prev_codes, shifted)
    codes_all = spread_blocks(codes, "tok")
    hidden_all = spread_blocks(hidden, "tok")
    source_all = spread_blocks(source, "tok")
    partial_value = (
        jnp.dot(codes_all, dec_own[0], preferred_element_type=jnp.float32)
        + jnp.dot(source_all, dec_prev[0], preferred_element_type=jnp.float32)
        - jnp.dot(hidden_all, w_down[0], preferred_element_type=jnp.float32)
    )
    groups = lax.axis_size("feat")
    terms = partial_value.reshape(groups, partial_value.shape[0] // groups, width)
    terms = lax.all_to_all(terms, "feat", split_axis=0, concat_axis=0, tiled=True)
    error_part = jnp.sum(terms, axis=0).astype(jnp.bfloat16)
    error_cols = lax.all_gather(error_part, "feat", axis=0, tiled=True)
    prev_back = summed_block(times(dec_prev[0].T), error_cols, "tok")
    later = passed_along(prev_back.astype(jnp.bfloat16), "layer", -1).astype(prev_back.dtype)
    own_back = summed_block(times(dec_own[0].T), error_cols, "tok")
    back = own_back + later
    factor = 1.0 / math.sqrt(height * lax.axis_size("tok"))
    pregrad = (back * keeper * (2.0 * active) * factor).astype(jnp.bfloat16)
    pregrad_all = spread_blocks(pregrad, "tok")
    grad_own = jnp.dot(codes_all.T, error_cols, preferred_element_type=jnp.float32) * factor
    grad_prev = jnp.dot(source_all.T, error_cols, preferred_element_type=jnp.float32) * factor
    grad_enc = jnp.dot(normed_cols.T, pregrad_all, preferred_element_type=jnp.float32)
    grad_bias = jnp.sum(pregrad_all.astype(jnp.float32), axis=0)
    return (grad_enc[None], grad_bias[None], grad_own[None], grad_prev[None])


def solution(mesh):
    in_specs = (
        P("layer", "tok", "feat"),
        P("layer", "feat"),
        P("tok", "feat"),
        P("layer", "tok", "feat"),
        P("layer", "tok", "feat"),
        P("layer", "tok", "feat"),
        P("layer", "feat", "tok"),
        P("layer", "tok", "feat"),
        P("layer", "feat"),
        P("layer", "feat", "tok"),
        P("layer", "feat", "tok"),
    )
    out_specs = (
        P("layer", "tok", "feat"),
        P("layer", "feat"),
        P("layer", "feat", "tok"),
        P("layer", "feat", "tok"),
    )
    return jax.shard_map(local, mesh=mesh, in_specs=in_specs, out_specs=out_specs, check_vma=False)
```
